32 devices in a mesh: space: 8 (over y, x, core), sample: 4 (over z).
Axes of the slice: x: 2, y: 2, z: 4, core: 2. Of those that a mesh axis runs over, the one named last changes fastest.
Arguments:
- volume: bfloat16 [4, 16, 32, 64, 128], P('sample', 'space'), may hold values from -6 to 6
- upstream: bfloat16 [4, 16, 32, 64, 128], P('sample', 'space'), may hold values from -6 to 6
- weight: bfloat16 [3456, 128], replicated, may hold values from -0.109375 to 0.109375
- first_moment: float32 [3456, 128], P('sample'), may hold values from -640 to 640
- second_moment: float32 [3456, 128], P('sample'), may hold values from 262.144 to 2621.44
Outputs:
- grad_volume: bfloat16 [4, 16, 32, 64, 128], P('sample', 'space')
- direction: float32 [3456, 128], P('sample')
The draws below stay inside these ranges and needn't reach their ends.
All inputs are finite; a program needn't handle non-finite values.
Results may differ from the reference program's by a relative error of at most 0.0039.
Values may be sent and summed in bfloat16 or wider, within the bound.
A program may use at most 64 MiB of HBM per device.

```python
import math
import jax
import jax.numpy as jnp
from jax import lax

C = 128
NY = 32
NX = 64
ADAM_STEP = 10
NZ = 16
SAMPLES = 4
KROWS = 3456


def spiked(entries, stream_key, source, target, blocks, factor):
    owner, partner = [(jnp.arange(entries.shape[axis_at]) // (entries.shape[axis_at] // blocks)).reshape([-1 if axis == axis_at else 1 for axis in range(entries.ndim)]) for axis_at in (source, target)]
    chosen = jax.random.permutation(stream_key, blocks)[partner]
    strong = (owner == chosen) | (owner == (partner + blocks // 2) % blocks)
    return jnp.where(strong, factor * entries, entries)


def level_of(own_key, shape, shards, least, largest):
    def one(position, parts):
        steps = jax.random.uniform(jax.random.fold_in(jax.random.fold_in(own_key, 6), position), (parts,), jnp.float32, least / len(shards), largest / len(shards))
        return jnp.repeat(jnp.exp(steps), shape[position] // parts).reshape((-1,) + (1,) * (len(shape) - position - 1))

    level = one(*shards[0])
    for cut in shards[1:]:
        level = level * one(*cut)
    return level


def noise(own_key, extent, spread, bound, split=(), kind=jnp.bfloat16):
    drawn = spread * jax.random.normal(own_key, extent, jnp.float32)
    if split:
        drawn = drawn * level_of(own_key, extent, split, -0.22, 0.18)
    return jnp.clip(drawn, -bound, bound).astype(kind)


def bell_draw_with(stream_key, shape, width, most, cuts, heavy, held_as=jnp.bfloat16):
    entries = width * jax.random.normal(stream_key, shape, jnp.float32)
    if cuts:
        entries = entries * level_of(stream_key, shape, cuts, -0.22, 0.18)
    return jnp.clip(spiked(entries, jax.random.fold_in(stream_key, 3), *heavy), -most, most).astype(held_as)


def setup_inputs(seed: int = 0) -> dict:
    keys = jax.random.split(jax.random.key(seed), 6)
    volume = noise(keys[0], (SAMPLES, NZ, NY, NX, C), 1.0, 6.0, ((0, 4), (1, 8)))
    upstream = bell_draw_with(keys[1], (SAMPLES, NZ, NY, NX, C), 1.0, 6.0, ((0, 4), (1, 8)), (1, 4, 8, 2.0))
    weight = noise(keys[2], (KROWS, C), (27 * C) ** -0.5, 0.109375)
    first_moment = noise(keys[3], (KROWS, C), (0.3 * (SAMPLES * NZ * NY * NX) ** 0.5), 640.0, ((0, 4),), jnp.float32)
    second_moment = jnp.clip(jnp.exp(math.log(2621.44) - 2.30258502 * jax.random.uniform(keys[4], (KROWS, C), jnp.float32) ** level_of(keys[4], (KROWS, C), ((0, 4),), -0.2, 0.2)), 262.144, 2621.44)
    return {"volume": volume, "upstream": upstream, "weight": weight, "first_moment": first_moment, "second_moment": second_moment}


beta_one = 0.9
beta_two = 0.999
eps_adam = 1e-08

def conv_same(field, kernel):
    return lax.conv_general_dilated(field, kernel, (1, 1, 1), ((1, 1), (1, 1), (1, 1)), dimension_numbers=('NDHWC', 'DHWIO', 'NDHWC'), preferred_element_type=jnp.float32)

def one_sample(kernel, flipped, pair):
    volume_one, upstream_one = pair
    channels = kernel.shape[3]
    field = volume_one[None]
    preact = conv_same(field, kernel)
    sigmoid_val = jax.nn.sigmoid(preact)
    slopes = sigmoid_val * (1.0 + preact * (1.0 - sigmoid_val))
    up_float = upstream_one[None].astype(jnp.float32)
    grad_pre = (up_float * slopes).astype(jnp.bfloat16)
    grad_volume = (up_float + conv_same(grad_pre, flipped)).astype(jnp.bfloat16)
    padded = jnp.pad(volume_one, ((1, 1), (1, 1), (1, 1), (0, 0)))
    flat_grad = grad_pre.reshape(-1, channels)

    def depth_rows(carry, depth):
        slab = lax.dynamic_slice_in_dim(padded, depth, NZ, 0)
        pieces = []
        for row_off in range(3):
            for col_off in range(3):
                shifted = slab[:, row_off:row_off + NY, col_off:col_off + NX, :].reshape(-1, channels)
                pieces.append(lax.dot_general(shifted, flat_grad, (((0,), (0,)), ((), ())), preferred_element_type=jnp.float32))
        return (carry, jnp.concatenate(pieces, axis=0))
    unused, blocks = lax.scan(depth_rows, jnp.zeros((), jnp.float32), jnp.arange(3, dtype=jnp.int32))
    return (grad_volume[0], blocks.reshape(-1, channels))

def reference(volume, upstream, weight, first_moment, second_moment):
    channels = weight.shape[1]
    kernel = weight.reshape(3, 3, 3, channels, channels)
    flipped = jnp.transpose(jnp.flip(kernel, (0, 1, 2)), (0, 1, 2, 4, 3))
    grad_volume, grads = lax.map(lambda pair: one_sample(kernel, flipped, pair), (volume, upstream))
    weight_grad = lax.optimization_barrier(jnp.sum(grads, axis=0))
    m_new = beta_one * first_moment + (1.0 - beta_one) * weight_grad
    v_new = beta_two * second_moment + (1.0 - beta_two) * weight_grad * weight_grad
    direction = m_new / (1.0 - beta_one ** ADAM_STEP) / (jnp.sqrt(v_new / (1.0 - beta_two ** ADAM_STEP)) + eps_adam)
    return (grad_volume, direction)
```

```python
import functools

import jax
import jax.numpy as jnp
from jax import lax
from jax.experimental import pallas as pl
from jax.experimental.pallas import tpu as pltpu
from jax.sharding import PartitionSpec as P

ADAM_STEP = 10

beta_one = 0.9
beta_two = 0.999
eps_adam = 1e-08

BF = jnp.bfloat16
F32 = jnp.float32
MESH = pl.DeviceIdType.MESH
CHUNKS = 4


def dot(a, b):
    return jnp.dot(a, b, preferred_element_type=F32)


def kernel(
    S, Z, h, q, e,
    vol, up, w, m_ref, v_ref,
    out, dirn,
    x3, g3, vt, wf, acc, gs, vh, gh, wg,
    s1, r1, a1, s2, r2, a2, s3, r3, a3, sx, rx, zs, zr, gsend, gbuf,
    vsend, vrecv, hsend, hrecv, st_send, st_recv, z_send, z_recv, g_send, g_recv,
):
    planes, ny, nx, ch = vol.shape
    three = 3 * ch
    nine = 3 * three
    step = ny // CHUNKS
    cells = ny * nx
    me = lax.axis_index("space")
    mz = lax.axis_index("sample")
    core = me % 2
    bx = (me // 2) % 2
    by = (me // 4) % 2
    group = me % 8
    base = me - group
    nxt = (me + 1) % S
    prv = (me + S - 1) % S
    extra = [b for b in (8, 16, 32, 64, 128) if b < S]

    def flip(bit):
        return me + bit - 2 * bit * ((me // bit) % 2)

    barrier = pltpu.get_barrier_semaphore()
    greet = [{"space": nxt}, {"space": prv}]
    greet += [{"space": base + (group + k) % 8} for k in range(1, 8)]
    greet += [{"space": flip(b)} for b in extra]
    greet += [{"sample": (mz + k) % Z} for k in range(1, Z)]
    for to in greet:
        pl.semaphore_signal(barrier, inc=1, device_id=to, device_id_type=MESH)
    pl.semaphore_wait(barrier, len(greet))

    def halo(src, dst, ssem, rsem, way, c):
        rows = pl.ds(c * step, step)
        plane = planes - 1 if way == 0 else 0
        return pltpu.make_async_remote_copy(
            src_ref=src.at[plane, rows],
            dst_ref=dst.at[way, rows],
            send_sem=ssem.at[way, c],
            recv_sem=rsem.at[way, c],
            device_id={"space": nxt if way == 0 else prv},
            device_id_type=MESH,
        )

    def has(way, sending):
        if (way == 0) == sending:
            return me < S - 1
        return me > 0

    def start_halo(src, dst, ssem, rsem, c):
        for way in range(2):
            @pl.when(has(way, True))
            def _():
                halo(src, dst, ssem, rsem, way, c).start()

    def wait_halo(src, dst, ssem, rsem, way, c):
        @pl.when(has(way, False))
        def _():
            halo(src, dst, ssem, rsem, way, c).wait_recv()

    def end_halo(src, dst, ssem, rsem):
        for way in range(2):
            @pl.when(has(way, True))
            def _():
                for c in range(CHUNKS):
                    halo(src, dst, ssem, rsem, way, c).wait_send()

    for c in range(CHUNKS):
        start_halo(vol, vh, vsend, vrecv, c)

    part = 4
    pos = lax.broadcasted_iota(jnp.int32, (part * nx, ch), 0) % nx

    def put3(dst, zi, row, val):
        n = part * nx
        at = pl.ds(row + 1, part)
        before = jnp.where(pos == 0, 0.0, pltpu.roll(val, 1, 0))
        after = jnp.where(pos == nx - 1, 0.0, pltpu.roll(val, n - 1, 0))
        dst[zi, at, :, 0:ch] = before.astype(BF).reshape(part, nx, ch)
        dst[zi, at, :, ch : 2 * ch] = val.astype(BF).reshape(part, nx, ch)
        dst[zi, at, :, 2 * ch :] = after.astype(BF).reshape(part, nx, ch)

    def fill(dst, zi, src, p, first, count):
        def one(i, _):
            row = first + i * part
            put3(dst, zi, row, src[p, pl.ds(row, part)].astype(F32).reshape(part * nx, ch))
            return 0
        lax.fori_loop(0, count // part, one, 0)

    def fill_halo(dst, src, way, first, count):
        zi = 0 if way == 0 else planes + 1

        @pl.when(has(way, False))
        def _():
            fill(dst, zi, src, way, first, count)

    for buf in (x3, g3):
        for zi in range(planes + 2):
            buf[zi, 0] = jnp.zeros((nx, three), BF)
            buf[zi, ny + 1] = jnp.zeros((nx, three), BF)
        for way in range(2):
            @pl.when(jnp.logical_not(has(way, False)))
            def _():
                zi = 0 if way == 0 else planes + 1

                def clear(i, _):
                    buf[zi, i + 1] = jnp.zeros((nx, three), BF)
                    return 0
                lax.fori_loop(0, ny, clear, 0)

    def turn(zi):
        def one(j, _):
            cols = 2 * ch // nx
            t = x3[zi, pl.ds(1 + cols * j, cols)].reshape(2 * ch, three)
            vt[zi, :, pl.ds(pl.multiple_of(j * 2 * ch, 2 * ch), 2 * ch)] = t.T
            return 0
        lax.fori_loop(0, cells // (2 * ch), one, 0)

    def taps(buf, zi, y0):
        return [buf[zi, pl.ds(y0 + dy, step)].reshape(step * nx, three) for dy in range(3)]

    def inner(buf, wt, zo):
        lo = max(1, zo)
        hi = min(planes, zo + 2)

        def one(c, _):
            y0 = c * step
            lhs = jnp.concatenate(sum([taps(buf, zi, y0) for zi in range(lo, hi + 1)], []), axis=1)
            acc[zo, pl.ds(y0, step)] = dot(lhs, wt[pl.ds((lo - zo) * nine, (hi + 1 - lo) * nine)]).reshape(step, nx, ch)
            return 0
        lax.fori_loop(0, CHUNKS, one, 0)

    def outer(buf, wt, zo, y0):
        res = acc[zo, pl.ds(y0, step)].reshape(step * nx, ch)
        for zi in (0, planes + 1):
            if zo <= zi <= zo + 2:
                res += dot(jnp.concatenate(taps(buf, zi, y0), axis=1), wt[pl.ds((zi - zo) * nine, nine)])
        return res

    for p in range(planes):
        fill(x3, p + 1, vol, p, 0, ny)
    for zo in range(planes):
        inner(x3, w, zo)
    for p in range(planes):
        turn(p + 1)

    def flip_w(t, _):
        src = pl.multiple_of((26 - t) * ch, ch)
        wf[pl.ds(pl.multiple_of(t * ch, ch), ch)] = w[pl.ds(src, ch)].T
        return 0
    lax.fori_loop(0, 27, flip_w, 0)

    def arrive(buf, raw, ssem, rsem, src, c):
        for way in range(2):
            wait_halo(src, raw, ssem, rsem, way, c)
            fill_halo(buf, raw, way, c * step, step)

    for c in range(CHUNKS):
        if c == 0:
            arrive(x3, vh, vsend, vrecv, vol, 0)
        if c + 1 < CHUNKS:
            arrive(x3, vh, vsend, vrecv, vol, c + 1)
        for zo in range(planes):
            y0 = c * step
            acc[zo, pl.ds(y0, step)] = outer(x3, w, zo, y0).reshape(step, nx, ch)

            def slope(i, _):
                at = pl.ds(y0 + i * part, part)
                pre = acc[zo, at].reshape(part * nx, ch)
                u = up[zo, at].astype(F32).reshape(part * nx, ch)
                s = jax.nn.sigmoid(pre)
                g = (u * (s * (1.0 + pre * (1.0 - s)))).astype(BF)
                gs[zo, at] = g.reshape(part, nx, ch)
                put3(g3, zo + 1, y0 + i * part, g.astype(F32))
                return 0
            lax.fori_loop(0, step // part, slope, 0)
        start_halo(gs, gh, hsend, hrecv, c)

    turn(0)
    turn(planes + 1)

    def grad(dz, _):
        for zo in range(planes):
            rhs = jnp.concatenate(
                [g3[zo + 1, 2 - dy : 2 - dy + ny, :, ch : 2 * ch].reshape(cells, ch) for dy in range(3)], axis=1
            )
            res = dot(vt[dz + zo], rhs)
            for dy in range(3):
                at = pl.ds(pl.multiple_of((dz * 3 + dy) * three, three), three)
                piece = res[:, dy * ch : (dy + 1) * ch]
                if zo == 0:
                    wg[at] = piece
                else:
                    wg[at] += piece
        return 0
    lax.fori_loop(0, 3, grad, 0)

    def swap(i, src, dst, to):
        return pltpu.make_async_remote_copy(
            src_ref=src, dst_ref=dst, send_sem=st_send.at[i], recv_sem=st_recv.at[i],
            device_id={"space": to}, device_id_type=MESH,
        )

    own = 2 * h

    def cut(ref, z, where, size, unit):
        return ref[z, pl.ds(pl.multiple_of(where, unit), size)]

    second = bx + core * (by - bx)
    third = by + core * (bx - by)
    to_second = flip(2) + core * (flip(4) - flip(2))
    to_third = flip(4) + core * (flip(2) - flip(4))

    for z in range(Z):
        s1[z] = wg[pl.ds(pl.multiple_of(z * own + h * (1 - core), 16), h)].astype(BF)
    first_swap = swap(0, s1, r1, flip(1))
    first_swap.start()
    inner(g3, wf, 0)
    first_swap.wait()
    for z in range(Z):
        a1[z] = wg[pl.ds(pl.multiple_of(z * own + h * core, 16), h)] + r1[z].astype(F32)
        s2[z] = cut(a1, z, (h - q) * (1 - second), q, 16).astype(BF)
    second_swap = swap(1, s2, r2, to_second)
    second_swap.start()
    for zo in range(1, planes):
        inner(g3, wf, zo)
    second_swap.wait()
    for z in range(Z):
        a2[z] = cut(a1, z, (h - q) * second, q, 16) + r2[z].astype(F32)
        s3[z] = cut(a2, z, e * (1 - third), e, 16).astype(BF)
    third_swap = swap(2, s3, r3, to_third)
    third_swap.start()

    def finish(zo):
        def one(c, _):
            y0 = c * step
            res = outer(g3, wf, zo, y0) + up[zo, pl.ds(y0, step)].astype(F32).reshape(step * nx, ch)
            out[zo, pl.ds(y0, step)] = res.astype(BF).reshape(step, nx, ch)
            return 0
        lax.fori_loop(0, CHUNKS, one, 0)

    third_swap.wait()
    for z in range(Z):
        a3[z] = cut(a2, z, e * third, e, 16) + r3[z].astype(F32)
    for i, bit in enumerate(extra):
        for z in range(Z):
            sx[i, z] = a3[z].astype(BF)
        more = swap(3 + i, sx.at[i], rx.at[i], flip(bit))
        more.start()
        more.wait()
        for z in range(Z):
            a3[z] = sx[i, z].astype(F32) + rx[i, z].astype(F32)

    def z_copy(k):
        return pltpu.make_async_remote_copy(
            src_ref=zs.at[(mz + k) % Z], dst_ref=zr.at[k - 1], send_sem=z_send.at[k - 1], recv_sem=z_recv.at[k - 1],
            device_id={"sample": (mz + k) % Z}, device_id_type=MESH,
        )

    for z in range(Z):
        zs[z] = a3[z].astype(BF)
    for k in range(1, Z):
        z_copy(k).start()

    for c in range(CHUNKS):
        arrive(g3, gh, hsend, hrecv, gs, c)
    finish(0)
    for k in range(1, Z):
        z_copy(k).wait()
    total = a3[mz]
    for k in range(1, Z):
        total += zr[k - 1].astype(F32)
    gsend[...] = total.astype(BF)

    def slot(g):
        c, x, y = g % 2, (g // 2) % 2, g // 4
        return 4 * c + 2 * (x + c * (y - x)) + (y + c * (x - y))

    def g_copy(k, place):
        return pltpu.make_async_remote_copy(
            src_ref=gsend, dst_ref=gbuf.at[place], send_sem=g_send.at[k - 1], recv_sem=g_recv.at[k - 1],
            device_id={"space": base + (group + k) % 8}, device_id_type=MESH,
        )

    for k in range(1, 8):
        g_copy(k, slot(group)).start()
    gbuf[slot(group)] = total.astype(BF)
    for zo in range(1, planes):
        finish(zo)
    for k in range(1, 8):
        g_copy(k, slot((group + 8 - k) % 8)).wait_recv()
    for i in range(8):
        at = pl.ds(h * (i // 4) + (h - q) * ((i // 2) % 2) + e * (i % 2), e)
        share = gbuf[i].astype(F32)
        m_new = beta_one * m_ref[at] + (1.0 - beta_one) * share
        v_new = beta_two * v_ref[at] + (1.0 - beta_two) * share * share
        dirn[at] = m_new / (1.0 - beta_one**ADAM_STEP) / (jnp.sqrt(v_new / (1.0 - beta_two**ADAM_STEP)) + eps_adam)
    for k in range(1, 8):
        g_copy(k, slot(group)).wait_send()
    end_halo(vol, vh, vsend, vrecv)
    end_halo(gs, gh, hsend, hrecv)


def body(S, Z, volume, upstream, weight, first_moment, second_moment):
    _, planes, ny, nx, ch = volume.shape
    rows = first_moment.shape[0]
    h = rows // 2
    q = -(-h // 64) * 32
    e = q // 2
    n_extra = max(1, S.bit_length() - 4)
    halo_shape = (2, ny, nx, ch)
    padded = (planes + 2, ny + 2, nx, 3 * ch)
    dma = pltpu.SemaphoreType.DMA
    vm = pltpu.VMEM
    grad_volume, direction = pl.pallas_call(
        functools.partial(kernel, S, Z, h, q, e),
        out_shape=(
            jax.ShapeDtypeStruct((planes, ny, nx, ch), BF),
            jax.ShapeDtypeStruct((rows, ch), F32),
        ),
        in_specs=[pl.BlockSpec(memory_space=pltpu.VMEM)] * 5,
        out_specs=(pl.BlockSpec(memory_space=pltpu.VMEM),) * 2,
        scratch_shapes=[
            vm(padded, BF),
            vm(padded, BF),
            vm((planes + 2, 3 * ch, ny * nx), BF),
            vm(weight.shape, BF),
            vm((planes, ny, nx, ch), F32),
            vm((planes, ny, nx, ch), BF),
            vm(halo_shape, BF),
            vm(halo_shape, BF),
            vm(weight.shape, F32),
            vm((Z, h, ch), BF),
            vm((Z, h, ch), BF),
            vm((Z, h, ch), F32),
            vm((Z, q, ch), BF),
            vm((Z, q, ch), BF),
            vm((Z, q, ch), F32),
            vm((Z, e, ch), BF),
            vm((Z, e, ch), BF),
            vm((Z, e, ch), F32),
            vm((n_extra, Z, e, ch), BF),
            vm((n_extra, Z, e, ch), BF),
            vm((Z, e, ch), BF),
            vm((Z - 1, e, ch), BF),
            vm((e, ch), BF),
            vm((8, e, ch), BF),
            dma((2, CHUNKS)),
            dma((2, CHUNKS)),
            dma((2, CHUNKS)),
            dma((2, CHUNKS)),
            dma((3 + n_extra,)),
            dma((3 + n_extra,)),
            dma((Z - 1,)),
            dma((Z - 1,)),
            dma((7,)),
            dma((7,)),
        ],
        compiler_params=pltpu.CompilerParams(
            collective_id=0, has_side_effects=True, vmem_limit_bytes=60 * 1024 * 1024
        ),
        name="block",
    )(volume[0], upstream[0], weight, first_moment, second_moment)
    return grad_volume[None], direction


def solution(mesh):
    return jax.shard_map(
        functools.partial(body, mesh.shape["space"], mesh.shape["sample"]),
        mesh=mesh,
        in_specs=(
            P("sample", "space", None, None, None),
            P("sample", "space", None, None, None),
            P(),
            P("sample", None),
            P("sample", None),
        ),
        out_specs=(P("sample", "space", None, None, None), P("sample", None)),
        check_vma=False,
    )
```

```python
import functools

import jax
import jax.numpy as jnp
from jax import lax
from jax.experimental import pallas as pl
from jax.experimental.pallas import tpu as pltpu
from jax.sharding import PartitionSpec as P

ADAM_STEP = 10

beta_one = 0.9
beta_two = 0.999
eps_adam = 1e-08

BF = jnp.bfloat16
F32 = jnp.float32
MESH = pl.DeviceIdType.MESH
CHUNKS = 4


def dot(a, b):
    return jnp.dot(a, b, preferred_element_type=F32)


def kernel(
    S, Z, h, q, e,
    vol_in, up_in, w_in, m_in, v_in,
    out_hbm, dirn,
    vol, up, w, m_ref, v_ref, out,
    x3, g3, vt, wf, acc, gs, vh, gh, wg,
    s1, r1, a1, s2, r2, a2, s3, r3, a3, sx, rx, zs, zr, gsend, gbuf,
    io_sem, vsend, vrecv, hsend, hrecv, st_send, st_recv, z_send, z_recv, g_send, g_recv,
):
    planes, ny, nx, ch = vol.shape
    loads = [
        pltpu.make_async_copy(a, b, io_sem.at[i])
        for i, (a, b) in enumerate(((vol_in, vol), (w_in, w), (up_in, up), (m_in, m_ref), (v_in, v_ref)))
    ]
    for load in loads:
        load.start()
    three = 3 * ch
    nine = 3 * three
    step = ny // CHUNKS
    cells = ny * nx
    me = lax.axis_index("space")
    mz = lax.axis_index("sample")
    core = me % 2
    bx = (me // 2) % 2
    by = (me // 4) % 2
    group = me % 8
    base = me - group
    nxt = (me + 1) % S
    prv = (me + S - 1) % S
    extra = [b for b in (8, 16, 32, 64, 128) if b < S]

    def flip(bit):
        return me + bit - 2 * bit * ((me // bit) % 2)

    barrier = pltpu.get_barrier_semaphore()
    greet = [{"space": nxt}, {"space": prv}]
    greet += [{"space": base + (group + k) % 8} for k in range(1, 8)]
    greet += [{"space": flip(b)} for b in extra]
    greet += [{"sample": (mz + k) % Z} for k in range(1, Z)]
    for to in greet:
        pl.semaphore_signal(barrier, inc=1, device_id=to, device_id_type=MESH)
    pl.semaphore_wait(barrier, len(greet))

    def halo(src, dst, ssem, rsem, way, c):
        rows = pl.ds(c * step, step)
        plane = planes - 1 if way == 0 else 0
        return pltpu.make_async_remote_copy(
            src_ref=src.at[plane, rows],
            dst_ref=dst.at[way, rows],
            send_sem=ssem.at[way, c],
            recv_sem=rsem.at[way, c],
            device_id={"space": nxt if way == 0 else prv},
            device_id_type=MESH,
        )

    def has(way, sending):
        if (way == 0) == sending:
            return me < S - 1
        return me > 0

    def start_halo(src, dst, ssem, rsem, c):
        for way in range(2):
            @pl.when(has(way, True))
            def _():
                halo(src, dst, ssem, rsem, way, c).start()

    def wait_halo(src, dst, ssem, rsem, way, c):
        @pl.when(has(way, False))
        def _():
            halo(src, dst, ssem, rsem, way, c).wait_recv()

    def end_halo(src, dst, ssem, rsem):
        for way in range(2):
            @pl.when(has(way, True))
            def _():
                for c in range(CHUNKS):
                    halo(src, dst, ssem, rsem, way, c).wait_send()

    relayed = range(CHUNKS // 2, CHUNKS) if S == 8 else ()
    senders, relays = (S // 2 - 1, S // 2), (S - 1, 0)

    def hop(way, c):
        rows = pl.ds(c * step, step)
        return pltpu.make_async_remote_copy(
            src_ref=vol_in.at[planes - 1 if way == 0 else 0, rows], dst_ref=vh.at[1 - way, rows],
            send_sem=vsend.at[way, c], recv_sem=vrecv.at[1 - way, c],
            device_id={"space": relays[way]}, device_id_type=MESH,
        )

    def pass_on(way, c):
        rows = pl.ds(c * step, step)
        return pltpu.make_async_remote_copy(
            src_ref=vh.at[1 - way, rows], dst_ref=vh.at[way, rows],
            send_sem=vsend.at[way, c], recv_sem=vrecv.at[way, c],
            device_id={"space": senders[1 - way]}, device_id_type=MESH,
        )

    for c in relayed:
        for way in range(2):
            @pl.when(me == senders[way])
            def _():
                hop(way, c).start()
    for c in range(CHUNKS):
        if c not in relayed:
            start_halo(vol_in, vh, vsend, vrecv, c)
            continue
        for way in range(2):
            @pl.when(jnp.logical_and(has(way, True), me != senders[way]))
            def _():
                halo(vol_in, vh, vsend, vrecv, way, c).start()

    part = 4
    pos = lax.broadcasted_iota(jnp.int32, (part * nx, ch), 0) % nx

    def put3(dst, zi, row, val):
        n = part * nx
        at = pl.ds(row + 1, part)
        before = jnp.where(pos == 0, 0.0, pltpu.roll(val, 1, 0))
        after = jnp.where(pos == nx - 1, 0.0, pltpu.roll(val, n - 1, 0))
        dst[zi, at, :, 0:ch] = before.astype(BF).reshape(part, nx, ch)
        dst[zi, at, :, ch : 2 * ch] = val.astype(BF).reshape(part, nx, ch)
        dst[zi, at, :, 2 * ch :] = after.astype(BF).reshape(part, nx, ch)

    def fill(dst, zi, src, p, first, count):
        def one(i, _):
            row = first + i * part
            put3(dst, zi, row, src[p, pl.ds(row, part)].astype(F32).reshape(part * nx, ch))
            return 0
        lax.fori_loop(0, count // part, one, 0)

    def fill_halo(dst, src, way, first, count):
        zi = 0 if way == 0 else planes + 1

        @pl.when(has(way, False))
        def _():
            fill(dst, zi, src, way, first, count)

    for buf in (x3, g3):
        for zi in range(planes + 2):
            buf[zi, 0] = jnp.zeros((nx, three), BF)
            buf[zi, ny + 1] = jnp.zeros((nx, three), BF)
        for way in range(2):
            @pl.when(jnp.logical_not(has(way, False)))
            def _():
                zi = 0 if way == 0 else planes + 1

                def clear(i, _):
                    buf[zi, i + 1] = jnp.zeros((nx, three), BF)
                    return 0
                lax.fori_loop(0, ny, clear, 0)

    def turn(zi):
        def one(j, _):
            cols = 2 * ch // nx
            t = x3[zi, pl.ds(1 + cols * j, cols)].reshape(2 * ch, three)
            vt[zi, :, pl.ds(pl.multiple_of(j * 2 * ch, 2 * ch), 2 * ch)] = t.T
            return 0
        lax.fori_loop(0, cells // (2 * ch), one, 0)

    def taps(buf, zi, y0):
        return [buf[zi, pl.ds(y0 + dy, step)].reshape(step * nx, three) for dy in range(3)]

    half = step // 2

    def inner(buf, wt):
        rhs = jnp.concatenate([wt[nine : 3 * nine], wt[0 : 2 * nine]], axis=1)

        def one(c, _):
            y0 = c * step
            lhs = jnp.concatenate(taps(buf, 1, y0) + taps(buf, 2, y0), axis=1)
            res = dot(lhs, rhs)
            at = pl.ds(c * half, half)
            for zo in range(2):
                acc[zo, at] = res[:, zo * ch : (zo + 1) * ch].reshape(half, 2, nx, ch)
            return 0
        lax.fori_loop(0, CHUNKS, one, 0)

    def outer(buf, wt, zo, c):
        zi = 3 * zo
        own_rows = wt[2 * zo * nine : (2 * zo + 1) * nine]
        gap = jnp.zeros((three, ch), BF)
        rhs = jnp.concatenate(
            [jnp.concatenate([own_rows, gap], axis=0), jnp.concatenate([gap, own_rows], axis=0)], axis=1
        )
        rows = buf[zi, pl.ds(c * step, step + 2)].reshape(half + 1, 2, nx, three)
        lhs = jnp.concatenate(
            [rows[d // 2 : d // 2 + half, d % 2].reshape(half * nx, three) for d in range(4)], axis=1
        )
        res = dot(lhs, rhs)
        at = pl.ds(c * half, half)
        for odd in range(2):
            acc[zo, at, odd] += res[:, odd * ch : (odd + 1) * ch].reshape(half, nx, ch)

    loads[0].wait()
    for p in range(planes):
        fill(x3, p + 1, vol, p, 0, ny)
    loads[1].wait()
    inner(x3, w)
    for c in relayed:
        for way in range(2):
            @pl.when(me == relays[way])
            def _():
                hop(way, c).wait_recv()
                pass_on(way, c).start()
    for p in range(planes):
        turn(p + 1)

    def flip_w(t, _):
        src = pl.multiple_of((26 - t) * ch, ch)
        wf[pl.ds(pl.multiple_of(t * ch, ch), ch)] = w[pl.ds(src, ch)].T
        return 0
    lax.fori_loop(0, 27, flip_w, 0)
    loads[2].wait()

    def arrive(buf, raw, ssem, rsem, src, c):
        for way in range(2):
            wait_halo(src, raw, ssem, rsem, way, c)
            fill_halo(buf, raw, way, c * step, step)

    for c in range(CHUNKS):
        if c == 0:
            arrive(x3, vh, vsend, vrecv, vol_in, 0)
        if c + 1 < CHUNKS:
            arrive(x3, vh, vsend, vrecv, vol_in, c + 1)
        for zo in range(planes):
            y0 = c * step
            outer(x3, w, zo, c)

            def slope(i, _):
                at = pl.ds(y0 + i * part, part)
                pre = acc[zo, pl.ds(y0 // 2 + i * (part // 2), part // 2)].reshape(part * nx, ch)
                u = up[zo, at].astype(F32).reshape(part * nx, ch)
                s = 0.5 + 0.5 * jnp.tanh(0.5 * pre)
                g = (u * (s * (1.0 + pre * (1.0 - s)))).astype(BF)
                gs[zo, at] = g.reshape(part, nx, ch)
                put3(g3, zo + 1, y0 + i * part, g.astype(F32))
                return 0
            lax.fori_loop(0, step // part, slope, 0)
        start_halo(gs, gh, hsend, hrecv, c)

    turn(0)
    turn(planes + 1)

    def grad(dz, _):
        for zo in range(planes):
            rhs = jnp.concatenate(
                [g3[zo + 1, 2 - dy : 2 - dy + ny, :, ch : 2 * ch].reshape(cells, ch) for dy in range(3)], axis=1
            )
            res = dot(vt[dz + zo], rhs)
            for dy in range(3):
                at = pl.ds(pl.multiple_of((dz * 3 + dy) * three, three), three)
                piece = res[:, dy * ch : (dy + 1) * ch]
                if zo == 0:
                    wg[at] = piece
                else:
                    wg[at] += piece
        return 0
    lax.fori_loop(0, 3, grad, 0)

    def swap(i, src, dst, to):
        return pltpu.make_async_remote_copy(
            src_ref=src, dst_ref=dst, send_sem=st_send.at[i], recv_sem=st_recv.at[i],
            device_id={"space": to}, device_id_type=MESH,
        )

    own = 2 * h

    def cut(ref, z, where, size, unit):
        return ref[z, pl.ds(pl.multiple_of(where, unit), size)]

    second = bx + core * (by - bx)
    third = by + core * (bx - by)
    to_second = flip(2) + core * (flip(4) - flip(2))
    to_third = flip(4) + core * (flip(2) - flip(4))

    def store(zo):
        return pltpu.make_async_copy(out.at[zo], out_hbm.at[zo], io_sem.at[5 + zo])

    def finish(zo):
        for c in range(CHUNKS):
            outer(g3, wf, zo, c)

            def one(i, _):
                row = c * step + i * part
                res = acc[zo, pl.ds(c * half + i * (part // 2), part // 2)].reshape(part, nx, ch)
                out[zo, pl.ds(row, part)] = (res + up[zo, pl.ds(row, part)].astype(F32)).astype(BF)
                return 0
            lax.fori_loop(0, step // part, one, 0)
        store(zo).start()

    for z in range(Z):
        s1[z] = wg[pl.ds(pl.multiple_of(z * own + h * (1 - core), 16), h)].astype(BF)
    first_swap = swap(0, s1, r1, flip(1))
    first_swap.start()
    first_swap.wait()
    for z in range(Z):
        a1[z] = wg[pl.ds(pl.multiple_of(z * own + h * core, 16), h)] + r1[z].astype(F32)
        s2[z] = cut(a1, z, (h - q) * (1 - second), q, 16).astype(BF)
    second_swap = swap(1, s2, r2, to_second)
    second_swap.start()
    inner(g3, wf)
    second_swap.wait()
    for z in range(Z):
        a2[z] = cut(a1, z, (h - q) * second, q, 16) + r2[z].astype(F32)
        s3[z] = cut(a2, z, e * (1 - third), e, 16).astype(BF)
    third_swap = swap(2, s3, r3, to_third)
    third_swap.start()

    for c in range(CHUNKS):
        arrive(g3, gh, hsend, hrecv, gs, c)
    third_swap.wait()
    for z in range(Z):
        a3[z] = cut(a2, z, e * third, e, 16) + r3[z].astype(F32)
    for i, bit in enumerate(extra):
        for z in range(Z):
            sx[i, z] = a3[z].astype(BF)
        more = swap(3 + i, sx.at[i], rx.at[i], flip(bit))
        more.start()
        more.wait()
        for z in range(Z):
            a3[z] = sx[i, z].astype(F32) + rx[i, z].astype(F32)

    def z_copy(k):
        return pltpu.make_async_remote_copy(
            src_ref=zs.at[(mz + k) % Z], dst_ref=zr.at[k - 1], send_sem=z_send.at[k - 1], recv_sem=z_recv.at[k - 1],
            device_id={"sample": (mz + k) % Z}, device_id_type=MESH,
        )

    for z in range(Z):
        zs[z] = a3[z].astype(BF)
    for k in range(1, Z):
        z_copy(k).start()

    finish(0)
    for k in range(1, Z):
        z_copy(k).wait()
    total = a3[mz]
    for k in range(1, Z):
        total += zr[k - 1].astype(F32)
    gsend[...] = total.astype(BF)

    def slot(g):
        c, x, y = g % 2, (g // 2) % 2, g // 4
        return 4 * c + 2 * (x + c * (y - x)) + (y + c * (x - y))

    def g_copy(k, place):
        return pltpu.make_async_remote_copy(
            src_ref=gsend, dst_ref=gbuf.at[place], send_sem=g_send.at[k - 1], recv_sem=g_recv.at[k - 1],
            device_id={"space": base + (group + k) % 8}, device_id_type=MESH,
        )

    for k in range(1, 8):
        g_copy(k, slot(group)).start()
    gbuf[slot(group)] = total.astype(BF)
    finish(1)
    for k in range(1, 8):
        g_copy(k, slot((group + 8 - k) % 8)).wait_recv()
    loads[3].wait()
    loads[4].wait()
    for i in range(8):
        at = pl.ds(h * (i // 4) + (h - q) * ((i // 2) % 2) + e * (i % 2), e)
        share = gbuf[i].astype(F32)
        m_new = beta_one * m_ref[at] + (1.0 - beta_one) * share
        v_new = beta_two * v_ref[at] + (1.0 - beta_two) * share * share
        dirn[at] = m_new / (1.0 - beta_one**ADAM_STEP) / (jnp.sqrt(v_new / (1.0 - beta_two**ADAM_STEP)) + eps_adam)
    for k in range(1, 8):
        g_copy(k, slot(group)).wait_send()
    for c in relayed:
        for way in range(2):
            @pl.when(me == relays[way])
            def _():
                pass_on(way, c).wait_send()
    for zo in range(planes):
        store(zo).wait()
    end_halo(vol_in, vh, vsend, vrecv)
    end_halo(gs, gh, hsend, hrecv)


def body(S, Z, volume, upstream, weight, first_moment, second_moment):
    _, planes, ny, nx, ch = volume.shape
    rows = first_moment.shape[0]
    assert planes == 2
    h = rows // 2
    q = -(-h // 64) * 32
    e = q // 2
    n_extra = max(1, S.bit_length() - 4)
    halo_shape = (2, ny, nx, ch)
    padded = (planes + 2, ny + 2, nx, 3 * ch)
    dma = pltpu.SemaphoreType.DMA
    vm = pltpu.VMEM
    grad_volume, direction = pl.pallas_call(
        functools.partial(kernel, S, Z, h, q, e),
        out_shape=(
            jax.ShapeDtypeStruct((planes, ny, nx, ch), BF),
            jax.ShapeDtypeStruct((rows, ch), F32),
        ),
        in_specs=[pl.BlockSpec(memory_space=pl.ANY)] * 5,
        out_specs=(pl.BlockSpec(memory_space=pl.ANY), pl.BlockSpec(memory_space=pltpu.VMEM)),
        scratch_shapes=[
            vm((planes, ny, nx, ch), BF),
            vm((planes, ny, nx, ch), BF),
            vm(weight.shape, BF),
            vm((rows, ch), F32),
            vm((rows, ch), F32),
            vm((planes, ny, nx, ch), BF),
            vm(padded, BF),
            vm(padded, BF),
            vm((planes + 2, 3 * ch, ny * nx), BF),
            vm(weight.shape, BF),
            vm((planes, ny // 2, 2, nx, ch), F32),
            vm((planes, ny, nx, ch), BF),
            vm(halo_shape, BF),
            vm(halo_shape, BF),
            vm(weight.shape, F32),
            vm((Z, h, ch), BF),
            vm((Z, h, ch), BF),
            vm((Z, h, ch), F32),
            vm((Z, q, ch), BF),
            vm((Z, q, ch), BF),
            vm((Z, q, ch), F32),
            vm((Z, e, ch), BF),
            vm((Z, e, ch), BF),
            vm((Z, e, ch), F32),
            vm((n_extra, Z, e, ch), BF),
            vm((n_extra, Z, e, ch), BF),
            vm((Z, e, ch), BF),
            vm((Z - 1, e, ch), BF),
            vm((e, ch), BF),
            vm((8, e, ch), BF),
            dma((5 + planes,)),
            dma((2, CHUNKS)),
            dma((2, CHUNKS)),
            dma((2, CHUNKS)),
            dma((2, CHUNKS)),
            dma((3 + n_extra,)),
            dma((3 + n_extra,)),
            dma((Z - 1,)),
            dma((Z - 1,)),
            dma((7,)),
            dma((7,)),
        ],
        compiler_params=pltpu.CompilerParams(
            collective_id=0, has_side_effects=True, vmem_limit_bytes=60 * 1024 * 1024
        ),
        name="block",
    )(volume[0], upstream[0], weight, first_moment, second_moment)
    return grad_volume[None], direction


def solution(mesh):
    return jax.shard_map(
        functools.partial(body, mesh.shape["space"], mesh.shape["sample"]),
        mesh=mesh,
        in_specs=(
            P("sample", "space", None, None, None),
            P("sample", "space", None, None, None),
            P(),
            P("sample", None),
            P("sample", None),
        ),
        out_specs=(P("sample", "space", None, None, None), P("sample", None)),
        check_vma=False,
    )
```

```python
import functools

import jax
import jax.numpy as jnp
from jax import lax
from jax.experimental import pallas as pl
from jax.experimental.pallas import tpu as pltpu
from jax.sharding import PartitionSpec as P

ADAM_STEP = 10

beta_one = 0.9
beta_two = 0.999
eps_adam = 1e-08

BF = jnp.bfloat16
F32 = jnp.float32
MESH = pl.DeviceIdType.MESH
CHUNKS = 4


def dot(a, b):
    return jnp.dot(a, b, preferred_element_type=F32)


def kernel(
    S, Z, h, q, e,
    vol_in, up_in, w_in, m_in, v_in,
    out_hbm, dirn,
    vol, up, w, m_ref, v_ref, out,
    x3, g3, vt, wf, acc, gs, vh, gh, wg,
    s1, r1, a1, s2, r2, a2, s3, r3, a3, sx, rx, zs, zr, gsend, gbuf,
    io_sem, vsend, vrecv, hsend, hrecv, st_send, st_recv, z_send, z_recv, g_send, g_recv,
):
    planes, ny, nx, ch = vol.shape
    loads = [
        pltpu.make_async_copy(a, b, io_sem.at[i])
        for i, (a, b) in enumerate(((vol_in, vol), (w_in, w), (up_in, up), (m_in, m_ref), (v_in, v_ref)))
    ]
    for load in loads:
        load.start()
    three = 3 * ch
    nine = 3 * three
    step = ny // CHUNKS
    cells = ny * nx
    me = lax.axis_index("space")
    mz = lax.axis_index("sample")
    core = me % 2
    bx = (me // 2) % 2
    by = (me // 4) % 2
    group = me % 8
    base = me - group
    nxt = (me + 1) % S
    prv = (me + S - 1) % S
    extra = [b for b in (8, 16, 32, 64, 128) if b < S]

    def flip(bit):
        return me + bit - 2 * bit * ((me // bit) % 2)

    barrier = pltpu.get_barrier_semaphore()
    greet = [{"space": nxt}, {"space": prv}]
    greet += [{"space": base + (group + k) % 8} for k in range(1, 8)]
    greet += [{"space": flip(b)} for b in extra]
    greet += [{"sample": (mz + k) % Z} for k in range(1, Z)]
    for to in greet:
        pl.semaphore_signal(barrier, inc=1, device_id=to, device_id_type=MESH)
    pl.semaphore_wait(barrier, len(greet))

    def halo(src, dst, ssem, rsem, way, c):
        rows = pl.ds(c * step, step)
        plane = planes - 1 if way == 0 else 0
        return pltpu.make_async_remote_copy(
            src_ref=src.at[plane, rows],
            dst_ref=dst.at[way, rows],
            send_sem=ssem.at[way, c],
            recv_sem=rsem.at[way, c],
            device_id={"space": nxt if way == 0 else prv},
            device_id_type=MESH,
        )

    def has(way, sending):
        if (way == 0) == sending:
            return me < S - 1
        return me > 0

    def start_halo(src, dst, ssem, rsem, c):
        for way in range(2):
            @pl.when(has(way, True))
            def _():
                halo(src, dst, ssem, rsem, way, c).start()

    def wait_halo(src, dst, ssem, rsem, way, c):
        @pl.when(has(way, False))
        def _():
            halo(src, dst, ssem, rsem, way, c).wait_recv()

    def end_halo(src, dst, ssem, rsem):
        for way in range(2):
            @pl.when(has(way, True))
            def _():
                for c in range(CHUNKS):
                    halo(src, dst, ssem, rsem, way, c).wait_send()

    relayed = range(CHUNKS // 2, CHUNKS) if S == 8 else ()
    senders, relays = (S // 2 - 1, S // 2), (S - 1, 0)

    def hop(way, c):
        rows = pl.ds(c * step, step)
        return pltpu.make_async_remote_copy(
            src_ref=vol_in.at[planes - 1 if way == 0 else 0, rows], dst_ref=vh.at[1 - way, rows],
            send_sem=vsend.at[way, c], recv_sem=vrecv.at[1 - way, c],
            device_id={"space": relays[way]}, device_id_type=MESH,
        )

    def pass_on(way, c):
        rows = pl.ds(c * step, step)
        return pltpu.make_async_remote_copy(
            src_ref=vh.at[1 - way, rows], dst_ref=vh.at[way, rows],
            send_sem=vsend.at[way, c], recv_sem=vrecv.at[way, c],
            device_id={"space": senders[1 - way]}, device_id_type=MESH,
        )

    for c in relayed:
        for way in range(2):
            @pl.when(me == senders[way])
            def _():
                hop(way, c).start()
    for c in range(CHUNKS):
        if c not in relayed:
            start_halo(vol_in, vh, vsend, vrecv, c)
            continue
        for way in range(2):
            @pl.when(jnp.logical_and(has(way, True), me != senders[way]))
            def _():
                halo(vol_in, vh, vsend, vrecv, way, c).start()

    part = 4
    pos = lax.broadcasted_iota(jnp.int32, (part * nx, ch), 0) % nx

    def put3(dst, zi, row, val):
        n = part * nx
        at = pl.ds(row + 1, part)
        before = jnp.where(pos == 0, 0.0, pltpu.roll(val, 1, 0))
        after = jnp.where(pos == nx - 1, 0.0, pltpu.roll(val, n - 1, 0))
        dst[zi, at, :, 0:ch] = before.astype(BF).reshape(part, nx, ch)
        dst[zi, at, :, ch : 2 * ch] = val.astype(BF).reshape(part, nx, ch)
        dst[zi, at, :, 2 * ch :] = after.astype(BF).reshape(part, nx, ch)

    def fill(dst, zi, src, p, first, count):
        def one(i, _):
            row = first + i * part
            put3(dst, zi, row, src[p, pl.ds(row, part)].astype(F32).reshape(part * nx, ch))
            return 0
        lax.fori_loop(0, count // part, one, 0, unroll=2)

    def fill_halo(dst, src, way, first, count):
        zi = 0 if way == 0 else planes + 1

        @pl.when(has(way, False))
        def _():
            fill(dst, zi, src, way, first, count)

    for buf in (x3, g3):
        for zi in range(planes + 2):
            buf[zi, 0] = jnp.zeros((nx, three), BF)
            buf[zi, ny + 1] = jnp.zeros((nx, three), BF)
        for way in range(2):
            @pl.when(jnp.logical_not(has(way, False)))
            def _():
                zi = 0 if way == 0 else planes + 1

                def clear(i, _):
                    buf[zi, i + 1] = jnp.zeros((nx, three), BF)
                    return 0
                lax.fori_loop(0, ny, clear, 0)

    def turn(zi):
        def one(j, _):
            cols = 2 * ch // nx
            t = x3[zi, pl.ds(1 + cols * j, cols)].reshape(2 * ch, three)
            vt[zi, :, pl.ds(pl.multiple_of(j * 2 * ch, 2 * ch), 2 * ch)] = t.T
            return 0
        lax.fori_loop(0, cells // (2 * ch), one, 0, unroll=4)

    def taps(buf, zi, y0):
        return [buf[zi, pl.ds(y0 + dy, step)].reshape(step * nx, three) for dy in range(3)]

    half = step // 2

    def inner(buf, wt):
        rhs = jnp.concatenate([wt[nine : 3 * nine], wt[0 : 2 * nine]], axis=1)

        def one(c, _):
            y0 = c * step
            lhs = jnp.concatenate(taps(buf, 1, y0) + taps(buf, 2, y0), axis=1)
            res = dot(lhs, rhs)
            at = pl.ds(c * half, half)
            for zo in range(2):
                acc[zo, at] = res[:, zo * ch : (zo + 1) * ch].reshape(half, 2, nx, ch)
            return 0
        lax.fori_loop(0, CHUNKS, one, 0)

    def outer(buf, wt, zo, c):
        zi = 3 * zo
        own_rows = wt[2 * zo * nine : (2 * zo + 1) * nine]
        gap = jnp.zeros((three, ch), BF)
        rhs = jnp.concatenate(
            [jnp.concatenate([own_rows, gap], axis=0), jnp.concatenate([gap, own_rows], axis=0)], axis=1
        )
        rows = buf[zi, pl.ds(c * step, step + 2)].reshape(half + 1, 2, nx, three)
        lhs = jnp.concatenate(
            [rows[d // 2 : d // 2 + half, d % 2].reshape(half * nx, three) for d in range(4)], axis=1
        )
        res = dot(lhs, rhs)
        at = pl.ds(c * half, half)
        for odd in range(2):
            acc[zo, at, odd] += res[:, odd * ch : (odd + 1) * ch].reshape(half, nx, ch)

    loads[0].wait()
    for p in range(planes):
        fill(x3, p + 1, vol, p, 0, ny)
    loads[1].wait()
    inner(x3, w)
    for c in relayed:
        for way in range(2):
            @pl.when(me == relays[way])
            def _():
                hop(way, c).wait_recv()
                pass_on(way, c).start()
    for p in range(planes):
        turn(p + 1)

    def flip_w(t, _):
        src = pl.multiple_of((26 - t) * ch, ch)
        wf[pl.ds(pl.multiple_of(t * ch, ch), ch)] = w[pl.ds(src, ch)].T
        return 0
    lax.fori_loop(0, 27, flip_w, 0, unroll=3)
    loads[2].wait()

    def arrive(buf, raw, ssem, rsem, src, c):
        for way in range(2):
            wait_halo(src, raw, ssem, rsem, way, c)
            fill_halo(buf, raw, way, c * step, step)

    for c in range(CHUNKS):
        if c == 0:
            arrive(x3, vh, vsend, vrecv, vol_in, 0)
        if c + 1 < CHUNKS:
            arrive(x3, vh, vsend, vrecv, vol_in, c + 1)
        for zo in range(planes):
            y0 = c * step
            outer(x3, w, zo, c)

            def slope(i, _):
                at = pl.ds(y0 + i * part, part)
                pre = acc[zo, pl.ds(y0 // 2 + i * (part // 2), part // 2)].reshape(part * nx, ch)
                u = up[zo, at].astype(F32).reshape(part * nx, ch)
                s = 0.5 + 0.5 * jnp.tanh(0.5 * pre)
                g = (u * (s * (1.0 + pre * (1.0 - s)))).astype(BF)
                gs[zo, at] = g.reshape(part, nx, ch)
                put3(g3, zo + 1, y0 + i * part, g.astype(F32))
                return 0
            lax.fori_loop(0, step // part, slope, 0, unroll=True)
        start_halo(gs, gh, hsend, hrecv, c)

    def g_rows(zo):
        return [g3[zo + 1, 2 - dy : 2 - dy + ny, :, ch : 2 * ch].reshape(cells, ch) for dy in range(3)]

    def put_grad(dz, res, at0, add):
        for dy in range(3):
            at = pl.ds((dz * 3 + dy) * three, three)
            piece = res[:, at0 + dy * ch : at0 + (dy + 1) * ch]
            if add:
                wg[at] += piece
            else:
                wg[at] = piece

    both = jnp.concatenate(g_rows(0) + g_rows(1), axis=1)
    for zi in (1, 2):
        res = dot(vt[zi], both)
        put_grad(zi, res, 0, False)
        put_grad(zi - 1, res, three, zi == 2)
    turn(0)
    put_grad(0, dot(vt[0], jnp.concatenate(g_rows(0), axis=1)), 0, True)
    turn(planes + 1)
    put_grad(2, dot(vt[3], jnp.concatenate(g_rows(1), axis=1)), 0, True)

    def swap(i, src, dst, to):
        return pltpu.make_async_remote_copy(
            src_ref=src, dst_ref=dst, send_sem=st_send.at[i], recv_sem=st_recv.at[i],
            device_id={"space": to}, device_id_type=MESH,
        )

    own = 2 * h

    def cut(ref, z, where, size, unit):
        return ref[z, pl.ds(pl.multiple_of(where, unit), size)]

    second = bx + core * (by - bx)
    third = by + core * (bx - by)
    to_second = flip(2) + core * (flip(4) - flip(2))
    to_third = flip(4) + core * (flip(2) - flip(4))

    def store(zo):
        return pltpu.make_async_copy(out.at[zo], out_hbm.at[zo], io_sem.at[5 + zo])

    def finish(zo):
        for c in range(CHUNKS):
            outer(g3, wf, zo, c)

            def one(i, _):
                row = c * step + i * part
                res = acc[zo, pl.ds(c * half + i * (part // 2), part // 2)].reshape(part, nx, ch)
                out[zo, pl.ds(row, part)] = (res + up[zo, pl.ds(row, part)].astype(F32)).astype(BF)
                return 0
            lax.fori_loop(0, step // part, one, 0)
        store(zo).start()

    for z in range(Z):
        s1[z] = wg[pl.ds(pl.multiple_of(z * own + h * (1 - core), 16), h)].astype(BF)
    first_swap = swap(0, s1, r1, flip(1))
    first_swap.start()
    first_swap.wait()
    for z in range(Z):
        a1[z] = wg[pl.ds(pl.multiple_of(z * own + h * core, 16), h)] + r1[z].astype(F32)
        s2[z] = cut(a1, z, (h - q) * (1 - second), q, 16).astype(BF)
    second_swap = swap(1, s2, r2, to_second)
    second_swap.start()
    inner(g3, wf)
    second_swap.wait()
    for z in range(Z):
        a2[z] = cut(a1, z, (h - q) * second, q, 16) + r2[z].astype(F32)
        s3[z] = cut(a2, z, e * (1 - third), e, 16).astype(BF)
    third_swap = swap(2, s3, r3, to_third)
    third_swap.start()

    for c in range(CHUNKS):
        arrive(g3, gh, hsend, hrecv, gs, c)
    third_swap.wait()
    for z in range(Z):
        a3[z] = cut(a2, z, e * third, e, 16) + r3[z].astype(F32)
    for i, bit in enumerate(extra):
        for z in range(Z):
            sx[i, z] = a3[z].astype(BF)
        more = swap(3 + i, sx.at[i], rx.at[i], flip(bit))
        more.start()
        more.wait()
        for z in range(Z):
            a3[z] = sx[i, z].astype(F32) + rx[i, z].astype(F32)

    def z_copy(k):
        return pltpu.make_async_remote_copy(
            src_ref=zs.at[(mz + k) % Z], dst_ref=zr.at[k - 1], send_sem=z_send.at[k - 1], recv_sem=z_recv.at[k - 1],
            device_id={"sample": (mz + k) % Z}, device_id_type=MESH,
        )

    for z in range(Z):
        zs[z] = a3[z].astype(BF)
    for k in range(1, Z):
        z_copy(k).start()

    finish(0)
    for k in range(1, Z):
        z_copy(k).wait()
    total = a3[mz]
    for k in range(1, Z):
        total += zr[k - 1].astype(F32)
    gsend[...] = total.astype(BF)

    def slot(g):
        c, x, y = g % 2, (g // 2) % 2, g // 4
        return 4 * c + 2 * (x + c * (y - x)) + (y + c * (x - y))

    def g_copy(k, place):
        return pltpu.make_async_remote_copy(
            src_ref=gsend, dst_ref=gbuf.at[place], send_sem=g_send.at[k - 1], recv_sem=g_recv.at[k - 1],
            device_id={"space": base + (group + k) % 8}, device_id_type=MESH,
        )

    for k in range(1, 8):
        g_copy(k, slot(group)).start()
    gbuf[slot(group)] = total.astype(BF)
    finish(1)
    for k in range(1, 8):
        g_copy(k, slot((group + 8 - k) % 8)).wait_recv()
    loads[3].wait()
    loads[4].wait()
    for i in range(8):
        at = pl.ds(h * (i // 4) + (h - q) * ((i // 2) % 2) + e * (i % 2), e)
        share = gbuf[i].astype(F32)
        m_new = beta_one * m_ref[at] + (1.0 - beta_one) * share
        v_new = beta_two * v_ref[at] + (1.0 - beta_two) * share * share
        dirn[at] = m_new / (1.0 - beta_one**ADAM_STEP) / (jnp.sqrt(v_new / (1.0 - beta_two**ADAM_STEP)) + eps_adam)
    for k in range(1, 8):
        g_copy(k, slot(group)).wait_send()
    for c in relayed:
        for way in range(2):
            @pl.when(me == relays[way])
            def _():
                pass_on(way, c).wait_send()
    for zo in range(planes):
        store(zo).wait()
    end_halo(vol_in, vh, vsend, vrecv)
    end_halo(gs, gh, hsend, hrecv)


def body(S, Z, volume, upstream, weight, first_moment, second_moment):
    _, planes, ny, nx, ch = volume.shape
    rows = first_moment.shape[0]
    assert planes == 2
    h = rows // 2
    q = -(-h // 64) * 32
    e = q // 2
    n_extra = max(1, S.bit_length() - 4)
    halo_shape = (2, ny, nx, ch)
    padded = (planes + 2, ny + 2, nx, 3 * ch)
    dma = pltpu.SemaphoreType.DMA
    vm = pltpu.VMEM
    grad_volume, direction = pl.pallas_call(
        functools.partial(kernel, S, Z, h, q, e),
        out_shape=(
            jax.ShapeDtypeStruct((planes, ny, nx, ch), BF),
            jax.ShapeDtypeStruct((rows, ch), F32),
        ),
        in_specs=[pl.BlockSpec(memory_space=pl.ANY)] * 5,
        out_specs=(pl.BlockSpec(memory_space=pl.ANY), pl.BlockSpec(memory_space=pltpu.VMEM)),
        scratch_shapes=[
            vm((planes, ny, nx, ch), BF),
            vm((planes, ny, nx, ch), BF),
            vm(weight.shape, BF),
            vm((rows, ch), F32),
            vm((rows, ch), F32),
            vm((planes, ny, nx, ch), BF),
            vm(padded, BF),
            vm(padded, BF),
            vm((planes + 2, 3 * ch, ny * nx), BF),
            vm(weight.shape, BF),
            vm((planes, ny // 2, 2, nx, ch), F32),
            vm((planes, ny, nx, ch), BF),
            vm(halo_shape, BF),
            vm(halo_shape, BF),
            vm(weight.shape, F32),
            vm((Z, h, ch), BF),
            vm((Z, h, ch), BF),
            vm((Z, h, ch), F32),
            vm((Z, q, ch), BF),
            vm((Z, q, ch), BF),
            vm((Z, q, ch), F32),
            vm((Z, e, ch), BF),
            vm((Z, e, ch), BF),
            vm((Z, e, ch), F32),
            vm((n_extra, Z, e, ch), BF),
            vm((n_extra, Z, e, ch), BF),
            vm((Z, e, ch), BF),
            vm((Z - 1, e, ch), BF),
            vm((e, ch), BF),
            vm((8, e, ch), BF),
            dma((5 + planes,)),
            dma((2, CHUNKS)),
            dma((2, CHUNKS)),
            dma((2, CHUNKS)),
            dma((2, CHUNKS)),
            dma((3 + n_extra,)),
            dma((3 + n_extra,)),
            dma((Z - 1,)),
            dma((Z - 1,)),
            dma((7,)),
            dma((7,)),
        ],
        compiler_params=pltpu.CompilerParams(
            collective_id=0, has_side_effects=True, vmem_limit_bytes=60 * 1024 * 1024
        ),
        name="block",
    )(volume[0], upstream[0], weight, first_moment, second_moment)
    return grad_volume[None], direction


def solution(mesh):
    return jax.shard_map(
        functools.partial(body, mesh.shape["space"], mesh.shape["sample"]),
        mesh=mesh,
        in_specs=(
            P("sample", "space", None, None, None),
            P("sample", "space", None, None, None),
            P(),
            P("sample", None),
            P("sample", None),
        ),
        out_specs=(P("sample", "space", None, None, None), P("sample", None)),
        check_vma=False,
    )
```
